128 devices in a mesh: sub: 8 (over x, core), tile: 16 (over y, z).
Axes of the slice: x: 4, y: 4, z: 4, core: 2. Of those that a mesh axis runs over, the one named last changes fastest.
Arguments:
- modes: bfloat16 [512, 768, 512], P(('sub', 'tile')), may hold values from -0.21875 to 0.21875
- coupling: bfloat16 [512, 8, 768, 128], P(('sub', 'tile')), may hold values from -0.796875 to 0.796875
- inv_eig: float32 [512, 512], P(('sub', 'tile')), may hold values from 0.1 to 1
- sub_rows: int32 [512], P(('sub', 'tile')), may hold values from 192 to 768
- adjacency: int32 [512, 8], P(('sub', 'tile')), may hold values from 0 to 2047, as said below
- base_mass: float32 [2048, 128, 128], P(('sub', 'tile')), may hold values from -0.5 to 0.5
- iface_modes: bfloat16 [262144, 2048], P(('sub', 'tile')), may hold values from -0.375 to 0.375
Outputs:
- reduced_mass: float32 [2048, 2048], P('sub', 'tile')
The draws below stay inside these ranges and needn't reach their ends.
Inputs may be any that keep to these rules, and one draw needn't show every extreme that they name: `adjacency`: interface block b is owned by device b // 16 in the order of the joined axes sub+tile. The substructures of one device link only to blocks whose owners have the same tile index; at most 8 links of one device go to blocks of one owner device, and on every device some owner receives exactly 8.
All inputs are finite; a program needn't handle non-finite values.
Results may differ from the reference program's by a relative error of at most 0.004.
Values may be sent and summed in bfloat16 or wider, within the bound.
A program may use at most 128 MiB of HBM per device.

```python
import math
import jax
import jax.numpy as jnp
from jax import lax

MODES = 512
IB = 128
KI = 2048
ROWS = 768
SUBS_DEV = 4
ADJ = 8
BLK_DEV = 16
CAP = 8
SUBS = 512
NB = 2048
N_SUB = 8
N_TILE = 16


def draw_sub_rows(key, part):
    first, second, third = jax.random.split(jax.random.fold_in(key, 11), 3)
    sizes = jax.random.randint(first, (SUBS,), ROWS // 4, ROWS + 1)
    upper = jax.random.randint(second, (), 0, SUBS)
    lower = (upper + 1 + jax.random.randint(third, (), 0, SUBS - 1)) % SUBS
    sizes = sizes.at[upper].set(ROWS).at[lower].set(ROWS // 4)
    return sizes.astype(jnp.int32)


def draw_adjacency(key, part):
    devices = N_SUB * N_TILE
    links = SUBS_DEV * ADJ
    pool = N_SUB * CAP

    def one_device(dev_key, device):
        kheavy, kperm, kmix, klocal = jax.random.split(dev_key, 4)
        heavy = jax.random.randint(kheavy, (), 0, N_SUB)
        owners = jax.random.permutation(kperm, pool) // CAP
        priority = jnp.where(owners == heavy, 0, pool) + jnp.arange(pool)
        chosen = owners[jnp.argsort(priority)][:links]
        chosen = chosen[jax.random.permutation(kmix, links)]
        local = jax.random.randint(klocal, (links,), 0, BLK_DEV)
        ids = (chosen * N_TILE + device % N_TILE) * BLK_DEV + local
        return ids.reshape(SUBS_DEV, ADJ)
    keys = jax.random.split(jax.random.fold_in(key, 23), devices)
    table = jax.vmap(one_device)(keys, jnp.arange(devices))
    return table.reshape(SUBS, ADJ).astype(jnp.int32)


def strengthened(result, stream_key, source, target, parts, factor):
    owner, partner = [(jnp.arange(result.shape[axis_at]) // (result.shape[axis_at] // parts)).reshape([-1 if axis == axis_at else 1 for axis in range(result.ndim)]) for axis_at in (source, target)]
    chosen = jax.random.permutation(stream_key, parts)[partner]
    strong = (owner == chosen) | (owner == (partner + parts // 2) % parts)
    return jnp.where(strong, factor * result, result)


def block_levels(own_key, extent, cuts, smallest, top_value):
    loudness, own = 1.0, jax.random.fold_in(own_key, 6)
    for axis_at, blocks in cuts:
        steps = jnp.exp(jax.random.uniform(jax.random.fold_in(own, axis_at), (blocks,), jnp.float32, smallest / len(cuts), top_value / len(cuts)))
        loudness = loudness * jnp.repeat(steps, extent[axis_at] // blocks).reshape([-1 if axis == axis_at else 1 for axis in range(len(extent))])
    return loudness


def normal_values(rng, extent, deviation, most, pieces=(), kind=jnp.bfloat16):
    loudness = block_levels(rng, extent, pieces, -0.22, 0.18) if pieces else 1.0
    values = jax.random.normal(rng, extent, jnp.float32) * deviation * loudness
    return jnp.minimum(jnp.maximum(values, -most), most).astype(kind)


def bell_draw_with(own_key, dims, deviation, limit, cuts, heavy, kind=jnp.bfloat16):
    array = deviation * jax.random.normal(own_key, dims, jnp.float32)
    if cuts:
        array = array * block_levels(own_key, dims, cuts, -0.22, 0.18)
    return jnp.clip(strengthened(array, jax.random.fold_in(own_key, 3), *heavy), -limit, limit).astype(kind)


def setup_inputs(seed: int = 0) -> dict:
    arg_keys = jax.random.split(jax.random.key(seed), 8)
    return {
        "modes": normal_values(arg_keys[0], (SUBS, ROWS, MODES), ROWS ** -0.5, 0.21875, ((0, 128),)),
        "coupling": normal_values(arg_keys[1], (SUBS, ADJ, ROWS, IB), 0.13, 0.796875, ((0, 128),)),
        "inv_eig": jnp.clip(jnp.exp(math.log(1.0) - 2.3025851 * jax.random.uniform(arg_keys[2], (SUBS, MODES), jnp.float32) ** block_levels(arg_keys[2], (SUBS, MODES), ((0, 128),), -0.2, 0.2)), 0.1, 1.0),
        "sub_rows": draw_sub_rows(jax.random.fold_in(arg_keys[7], 71), 0),
        "adjacency": draw_adjacency(jax.random.fold_in(arg_keys[7], 71), 0),
        "base_mass": normal_values(arg_keys[5], (NB, IB, IB), IB ** -0.5, 0.5, ((0, 128),), jnp.float32),
        "iface_modes": bell_draw_with(arg_keys[6], (NB * IB, KI), 0.015, 0.375, ((0, 128),), (0, 1, 128, 5.5)),
    }


def reduce_one(item):
    masked_s, coupling_s, inv_s = item
    reduced = jnp.einsum("rm,arc->amc", masked_s.astype(jnp.float32), coupling_s.astype(jnp.float32))
    reduced_b = reduced.astype(jnp.bfloat16)
    weighted = (reduced * inv_s[None, :, None]).astype(jnp.bfloat16)
    contrib = jnp.einsum("amc,amd->acd", weighted.astype(jnp.float32), reduced_b.astype(jnp.float32))
    return contrib.astype(jnp.bfloat16)


def reference(modes, coupling, inv_eig, sub_rows, adjacency, base_mass, iface_modes):
    live = (jnp.arange(ROWS, dtype=jnp.int32)[None, :] < sub_rows[:, None]).astype(jnp.bfloat16)
    masked = modes * live[:, :, None]
    contrib = lax.map(reduce_one, (masked, coupling, inv_eig))
    flat_links = contrib.reshape(SUBS * ADJ, IB, IB).astype(jnp.float32)
    assembled = base_mass + jax.ops.segment_sum(flat_links, adjacency.reshape(-1), num_segments=NB)
    mass_rounded = assembled.astype(jnp.bfloat16)
    psi_blocks = iface_modes.reshape(NB, IB, KI)

    def accumulate(total, item):
        mass_b, psi_b = item
        image = jnp.dot(mass_b, psi_b, preferred_element_type=jnp.float32).astype(jnp.bfloat16)
        return total + jnp.dot(psi_b.T, image, preferred_element_type=jnp.float32), None

    reduced_mass, unused = lax.scan(accumulate, jnp.zeros((KI, KI), jnp.float32), (mass_rounded, psi_blocks))
    return reduced_mass
```

```python
import jax
import jax.numpy as jnp
from jax import lax
from jax.experimental import pallas as pl
from jax.experimental.pallas import tpu as pltpu
from jax.sharding import PartitionSpec as P

MESH = pl.DeviceIdType.MESH
F32 = jnp.float32
BF16 = jnp.bfloat16
ORDER = (2, 1, 3, 0)
PARTS = ((0, 96), (96, 80), (176, 80))


def contrib_kernel(rows_ref, adj_ref, modes_ref, coup_ref, inv_ref, out_ref, ct, rtb, wt):
    s = pl.program_id(0)
    links = coup_ref.shape[1]
    rows, modes = modes_ref.shape[1:]
    block = coup_ref.shape[3]

    @pl.when(s == 0)
    def _():
        @pl.loop(0, out_ref.shape[0])
        def _(b):
            out_ref[b] = jnp.zeros(out_ref.shape[1:], BF16)

    for a in range(links):
        ct[a * block : (a + 1) * block, :] = coup_ref[0, a].T
    live = lax.broadcasted_iota(jnp.int32, (rows, modes), 0) < rows_ref[s]
    masked = jnp.where(live, modes_ref[0].astype(F32), 0.0).astype(BF16)
    reduced = jnp.dot(ct[...], masked, preferred_element_type=F32)
    rtb[...] = reduced.astype(BF16)
    wt[...] = (reduced * inv_ref[0]).astype(BF16)
    for a in range(links):
        own = slice(a * block, (a + 1) * block)
        contrib = lax.dot_general(
            wt[own, :], rtb[own, :], (((1,), (1,)), ((), ())), preferred_element_type=F32
        ).astype(BF16)
        ident = adj_ref[s, a]
        place = (ident // 256) * 16 + ident % 16
        out_ref[place] = (out_ref[place].astype(F32) + contrib.astype(F32)).astype(BF16)


def contributions(modes, coupling, inv_eig, sub_rows, adjacency):
    subs, rows, width = modes.shape
    links, block = coupling.shape[1], coupling.shape[3]
    return pl.pallas_call(
        contrib_kernel,
        out_shape=jax.ShapeDtypeStruct((128, block, block), BF16),
        grid_spec=pltpu.PrefetchScalarGridSpec(
            num_scalar_prefetch=2,
            grid=(subs,),
            in_specs=[
                pl.BlockSpec((1, rows, width), lambda s, *_: (s, 0, 0)),
                pl.BlockSpec((1, links, rows, block), lambda s, *_: (s, 0, 0, 0)),
                pl.BlockSpec((1, 1, width), lambda s, *_: (s, 0, 0)),
            ],
            out_specs=pl.BlockSpec((128, block, block), lambda s, *_: (0, 0, 0)),
            scratch_shapes=[
                pltpu.VMEM((links * block, rows), BF16),
                pltpu.VMEM((links * block, width), BF16),
                pltpu.VMEM((links * block, width), BF16),
            ],
        ),
        compiler_params=pltpu.CompilerParams(vmem_limit_bytes=48 * 1024 * 1024),
    )(sub_rows, adjacency, modes, coupling, inv_eig.reshape(subs, 1, width))


SCRATCH = {
    "dm": pltpu.VMEM((4, 16, 128, 128), BF16),
    "rc": pltpu.VMEM((4, 16, 128, 128), BF16),
    "mra": pltpu.VMEM((16, 128, 128), BF16),
    "mrb": pltpu.VMEM((2, 16, 128, 128), BF16),
    "base_v": pltpu.VMEM((16, 128, 128), F32),
    "mb": pltpu.VMEM((16, 128, 128), BF16),
    "psi_v": pltpu.VMEM((2048, 2048), BF16),
    "psit": pltpu.VMEM((2, 1024, 2048), BF16),
    "img": pltpu.VMEM((8, 2048, 256), BF16),
    "ps": pltpu.VMEM((8, 1024, 256), BF16),
    "rp": pltpu.VMEM((8, 1024, 256), BF16),
}
for part, (_, high) in enumerate(PARTS):
    SCRATCH[f"pb{part}"] = pltpu.VMEM((4, 4, 4, high, 128), BF16)
    SCRATCH[f"ra{part}"] = pltpu.VMEM((4, 4, high, 128), BF16)
    SCRATCH[f"rb{part}"] = pltpu.VMEM((2, 4, 4, high, 128), BF16)
    SCRATCH[f"q2{part}"] = pltpu.VMEM((4, 4, high, 128), F32)
    SCRATCH[f"sa{part}"] = pltpu.VMEM((4, high, 128), F32)
    SCRATCH[f"sb{part}"] = pltpu.VMEM((2, 4, high, 128), F32)
    SCRATCH[f"q3{part}"] = pltpu.VMEM((4, high, 128), F32)
    SCRATCH[f"ta{part}"] = pltpu.VMEM((high, 128), F32)
    SCRATCH[f"tb{part}"] = pltpu.VMEM((2, high, 128), F32)
MESSAGES = 128
SCRATCH["psem"] = pltpu.SemaphoreType.DMA((8,))
SCRATCH["lsem"] = pltpu.SemaphoreType.DMA((8,))
SCRATCH["ssem"] = pltpu.SemaphoreType.DMA((MESSAGES,))
SCRATCH["rsem"] = pltpu.SemaphoreType.DMA((MESSAGES,))


def project_kernel(d_ref, base_ref, psi_ref, out_ref, *scratch):
    v = dict(zip(SCRATCH, scratch))
    dm, rc, mra, mrb, mb = v["dm"], v["rc"], v["mra"], v["mrb"], v["mb"]
    psi_v, psit, img, ps, rp = v["psi_v"], v["psit"], v["img"], v["ps"], v["rp"]
    ssem, rsem, lsem, psem = v["ssem"], v["rsem"], v["lsem"], v["psem"]
    pb, ra, rb = ([v[f"{n}{p}"] for p in range(3)] for n in ("pb", "ra", "rb"))
    q2, sa, sb = ([v[f"{n}{p}"] for p in range(3)] for n in ("q2", "sa", "sb"))
    q3, ta, tb = ([v[f"{n}{p}"] for p in range(3)] for n in ("q3", "ta", "tb"))

    sub, tile = lax.axis_index("sub"), lax.axis_index("tile")
    core, x = lax.rem(sub, 2), lax.div(sub, 2)
    y, z = lax.div(tile, 4), lax.rem(tile, 4)
    partner = {"sub": x * 2 + 1 - core, "tile": tile}

    def step(axis, d):
        if axis == "x":
            return {"sub": lax.rem(x + d, 4) * 2 + core, "tile": tile}
        if axis == "y":
            return {"sub": sub, "tile": lax.rem(y + d, 4) * 4 + z}
        return {"sub": sub, "tile": y * 4 + lax.rem(z + d, 4)}

    plus = {a: step(a, 1) for a in "xyz"}
    minus = {a: step(a, 3) for a in "xyz"}

    barrier = pltpu.get_barrier_semaphore()
    peers = [partner] + [plus[a] for a in "xyz"] + [minus[a] for a in "xyz"]
    for peer in peers:
        pl.semaphore_signal(barrier, inc=1, device_id=peer, device_id_type=MESH)

    def psi_copy(k):
        rows = pl.ds(pl.multiple_of(k * 256, 256), 256)
        return pltpu.make_async_copy(psi_ref.at[rows], psi_v.at[rows], psem.at[k])

    own_d = []
    for i, d in enumerate(ORDER):
        at = lax.rem(x + d, 4) * 2 + core
        own_d.append(pltpu.make_async_copy(d_ref.at[at], dm.at[i], lsem.at[i]))
        own_d[-1].start()
    base_copy = pltpu.make_async_copy(base_ref, v["base_v"], lsem.at[4])

    pl.semaphore_wait(barrier, len(peers))

    count = [0]
    sent = []

    def message(src, dst, device):
        k = count[0]
        count[0] += 1
        copy = pltpu.make_async_remote_copy(
            src_ref=src,
            dst_ref=dst,
            send_sem=ssem.at[k],
            recv_sem=rsem.at[k],
            device_id=device,
            device_id_type=MESH,
        )
        copy.start()
        sent.append(copy)
        return copy

    from_core = []
    for i, d in enumerate(ORDER):
        at = lax.rem(x + d, 4) * 2 + 1 - core
        from_core.append(message(d_ref.at[at], rc.at[i], partner))
    for k in range(8):
        psi_copy(k).start()
    base_copy.start()

    def add_blocks(dst, src, blocks):
        @pl.loop(0, blocks)
        def _(b):
            dst[b] = (dst[b].astype(F32) + src[b].astype(F32)).astype(BF16)

    def transpose_rows(first, last):
        @pl.loop(first, last)
        def _(k):
            psi_copy(k).wait()
            rows = pl.ds(pl.multiple_of(k * 256, 256), 256)
            for cc in range(2):
                for i, d in enumerate(ORDER):
                    band = lax.rem(x + d, 4) * 2 + (core if cc else 1 - core)
                    cols = pl.ds(pl.multiple_of(band * 256, 256), 256)
                    psit[cc, i * 256 : (i + 1) * 256, rows] = psi_v[rows, cols].T

    for i in range(4):
        own_d[i].wait()
        from_core[i].wait_recv()
        add_blocks(dm.at[i], rc.at[i], 16)
        if i == 0:
            m_ap = message(dm.at[0, 0:8], mra.at[0:8], plus["x"])
            m_am = message(dm.at[0, 8:16], mra.at[8:16], minus["x"])
        if i == 1:
            m_bp = message(dm.at[1, 8:16], mrb.at[0, 8:16], plus["x"])
        if i == 2:
            m_bm = message(dm.at[2, 0:8], mrb.at[1, 0:8], minus["x"])
    m_ap.wait_recv()
    add_blocks(dm.at[1, 0:8], mra.at[0:8], 8)
    m_cp = message(dm.at[1, 0:8], mrb.at[0, 0:8], plus["x"])
    m_am.wait_recv()
    add_blocks(dm.at[2, 8:16], mra.at[8:16], 8)
    m_cm = message(dm.at[2, 8:16], mrb.at[1, 8:16], minus["x"])
    transpose_rows(0, 8)
    base_copy.wait()
    for m in (m_bp, m_bm, m_cp, m_cm):
        m.wait_recv()

    @pl.loop(0, 16)
    def _(b):
        total = v["base_v"][b] + dm[3, b].astype(F32)
        total = total + (mrb[0, b].astype(F32) + mrb[1, b].astype(F32))
        mb[b] = total.astype(BF16)

    @pl.loop(0, 16)
    def _(b):
        rows = pl.ds(pl.multiple_of(b * 128, 128), 128)
        mass = mb[b]
        for u in range(8):
            iy, n = divmod(u, 2)
            tiles = []
            for t in range(2):
                at = lax.rem(y + ORDER[iy], 4) * 4 + lax.rem(z + ORDER[2 * n + t], 4)
                tiles.append(psi_v[rows, pl.ds(pl.multiple_of(at * 128, 128), 128)])
            rhs = jnp.concatenate(tiles, axis=1)
            img[u, rows, :] = jnp.dot(mass, rhs, preferred_element_type=F32).astype(BF16)

    half_base = count[0]
    count[0] += 8

    def half_copy(u):
        return pltpu.make_async_remote_copy(
            src_ref=ps.at[u],
            dst_ref=rp.at[u],
            send_sem=ssem.at[half_base + u],
            recv_sem=rsem.at[half_base + u],
            device_id=partner,
            device_id_type=MESH,
        )

    @pl.loop(0, 8)
    def _(u):
        ps[u] = jnp.dot(psit[0], img[u], preferred_element_type=F32).astype(BF16)
        half_copy(u).start()

    axes = (("y", "z", "x"), ("x", "y", "z"), ("z", "x", "y"))
    first_a = {}
    first_b = {}

    def merge(p, r, c):
        ref, got = pb[p].at[r, c], ra[p].at[r]
        ref[...] = (ref[...].astype(F32) + got[...].astype(F32)).astype(BF16)

    def late(p, r):
        a = axes[p][0]
        first_a[p, r].wait_recv()
        side = 0 if r < 2 else 1
        merge(p, r, 1 + side)
        to = (plus, minus)[side][a]
        first_b[p, r, side] = message(pb[p].at[r, 1 + side], rb[p].at[side, r], to)

    for iy in range(4):
        @pl.loop(0, 2)
        def _(n):
            u = iy * 2 + n
            half_copy(u).wait_recv()
            acc = jnp.dot(psit[1], img[u], preferred_element_type=F32)
            acc = acc + rp[u].astype(F32)
            for ix in range(4):
                for t in range(2):
                    iz = 2 * n + t
                    for p, (off, high) in enumerate(PARTS):
                        value = acc[
                            ix * 256 + off : ix * 256 + off + high, t * 128 : (t + 1) * 128
                        ].astype(BF16)
                        if p == 2:
                            pb[p][iy, iz, ix] = value
                        else:
                            pb[p][iy, ix, iz] = value

        if iy == 0:
            first_a[0, 0] = message(pb[0].at[0, 0:2], ra[0].at[0:2], plus["y"])
            first_a[0, 1] = message(pb[0].at[0, 2:4], ra[0].at[2:4], minus["y"])
        for p in (1, 2):
            a = axes[p][0]
            to = (plus if iy < 2 else minus)[a]
            first_a[p, iy] = message(pb[p].at[iy, 0], ra[p].at[iy], to)
            side = 1 if iy < 2 else 0
            to = (plus, minus)[side][a]
            first_b[p, iy, side] = message(pb[p].at[iy, 1 + side], rb[p].at[side, iy], to)
        if iy in (1, 2):
            side = iy - 1
            first_a[0, side].wait_recv()
            for ix in (2 * side, 2 * side + 1):
                ref, got = pb[0].at[iy, ix], ra[0].at[ix]
                ref[...] = (ref[...].astype(F32) + got[...].astype(F32)).astype(BF16)
            to = (plus, minus)[side]["y"]
            first_b[0, 0, side] = message(pb[0].at[iy], rb[0].at[side], to)
        if iy >= 1:
            late(1, iy - 1)
            late(2, iy - 1)
    late(1, 3)
    late(2, 3)

    for side in range(2):
        first_b[0, 0, side].wait_recv()
    for ix in range(4):
        for iz in range(4):
            q2[0][iz, ix] = pb[0][3, ix, iz].astype(F32) + (
                rb[0][0, ix, iz].astype(F32) + rb[0][1, ix, iz].astype(F32)
            )
    for iy in range(4):
        for p in (1, 2):
            for side in range(2):
                first_b[p, iy, side].wait_recv()
            for j in range(4):
                total = pb[p][iy, 3, j].astype(F32) + (
                    rb[p][0, iy, j].astype(F32) + rb[p][1, iy, j].astype(F32)
                )
                if p == 1:
                    q2[p][iy, j] = total
                else:
                    q2[p][j, iy] = total

    second = {}
    for p in range(3):
        up, down = plus[axes[p][1]], minus[axes[p][1]]
        second[p, "ap"] = message(q2[p].at[0, 0:2], sa[p].at[0:2], up)
        second[p, "am"] = message(q2[p].at[0, 2:4], sa[p].at[2:4], down)
        second[p, "bp"] = message(q2[p].at[1, 2:4], sb[p].at[0, 2:4], up)
        second[p, "bm"] = message(q2[p].at[2, 0:2], sb[p].at[1, 0:2], down)
    for p in range(3):
        up, down = plus[axes[p][1]], minus[axes[p][1]]
        second[p, "ap"].wait_recv()
        q2[p][1, 0:2] = q2[p][1, 0:2] + sa[p][0:2]
        second[p, "cp"] = message(q2[p].at[1, 0:2], sb[p].at[0, 0:2], up)
        second[p, "am"].wait_recv()
        q2[p][2, 2:4] = q2[p][2, 2:4] + sa[p][2:4]
        second[p, "cm"] = message(q2[p].at[2, 2:4], sb[p].at[1, 2:4], down)

    third = {}
    for p, (off, high) in enumerate(PARTS):
        for name in ("bp", "bm", "cp", "cm"):
            second[p, name].wait_recv()
        q3[p][...] = q2[p][3] + (sb[p][0] + sb[p][1])
        up, down = plus[axes[p][2]], minus[axes[p][2]]
        cut = high // 2
        third[p, "ap"] = message(q3[p].at[0, 0:cut], ta[p].at[0:cut], up)
        third[p, "am"] = message(q3[p].at[0, cut:high], ta[p].at[cut:high], down)
        third[p, "bp"] = message(q3[p].at[1, cut:high], tb[p].at[0, cut:high], up)
        third[p, "bm"] = message(q3[p].at[2, 0:cut], tb[p].at[1, 0:cut], down)
    for p, (off, high) in enumerate(PARTS):
        up, down = plus[axes[p][2]], minus[axes[p][2]]
        cut = high // 2
        third[p, "ap"].wait_recv()
        q3[p][1, 0:cut] = q3[p][1, 0:cut] + ta[p][0:cut]
        third[p, "cp"] = message(q3[p].at[1, 0:cut], tb[p].at[0, 0:cut], up)
        third[p, "am"].wait_recv()
        q3[p][2, cut:high] = q3[p][2, cut:high] + ta[p][cut:high]
        third[p, "cm"] = message(q3[p].at[2, cut:high], tb[p].at[1, cut:high], down)
    for p, (off, high) in enumerate(PARTS):
        for name in ("bp", "bm", "cp", "cm"):
            third[p, name].wait_recv()
        out_ref[off : off + high, :] = q3[p][3] + (tb[p][0] + tb[p][1])

    for copy in sent:
        copy.wait_send()

    @pl.loop(0, 8)
    def _(u):
        half_copy(u).wait_send()

    assert count[0] <= MESSAGES


def project(dense, base_mass, iface_modes):
    hbm = pl.BlockSpec(memory_space=pl.ANY)
    return pl.pallas_call(
        project_kernel,
        out_shape=jax.ShapeDtypeStruct((256, 128), F32),
        in_specs=[hbm, hbm, hbm],
        out_specs=pl.BlockSpec(memory_space=pltpu.VMEM),
        scratch_shapes=list(SCRATCH.values()),
        compiler_params=pltpu.CompilerParams(
            collective_id=0, has_side_effects=True, vmem_limit_bytes=67043328
        ),
    )(dense, base_mass, iface_modes)


def on_device(modes, coupling, inv_eig, sub_rows, adjacency, base_mass, iface_modes):
    dense = contributions(modes, coupling, inv_eig, sub_rows, adjacency)
    return project(dense.reshape(8, 16, 128, 128), base_mass, iface_modes)


def solution(mesh):
    placed = (
        P(("sub", "tile"), None, None),
        P(("sub", "tile"), None, None, None),
        P(("sub", "tile"), None),
        P(("sub", "tile")),
        P(("sub", "tile"), None),
        P(("sub", "tile"), None, None),
        P(("sub", "tile"), None),
    )
    return jax.shard_map(
        on_device, mesh=mesh, in_specs=placed, out_specs=P("sub", "tile"), check_vma=False
    )
```

```python
import jax
import jax.numpy as jnp
from jax import lax
from jax.experimental import pallas as pl
from jax.experimental.pallas import tpu as pltpu
from jax.sharding import PartitionSpec as P

MESH = pl.DeviceIdType.MESH
F32 = jnp.float32
BF16 = jnp.bfloat16
ORDER = (2, 1, 3, 0)
PACKED = 16 * 64 + 16


def contrib_kernel(rows_ref, adj_ref, modes_ref, coup_ref, inv_ref, out_ref, ct, rtb, wt, dg):
    s = pl.program_id(0)
    links = coup_ref.shape[1]
    rows, modes = modes_ref.shape[1:]
    block = coup_ref.shape[3]
    half = block // 2

    @pl.when(s == 0)
    def _():
        dg[...] = jnp.zeros(dg.shape, F32)
        for owner in range(8):
            @pl.loop(0, PACKED // 80)
            def _(b):
                at = pl.ds(pl.multiple_of(b * 80, 16), 80)
                out_ref[owner, at, :] = jnp.zeros((80, block), BF16)

    for a in range(links):
        ct[a * block : (a + 1) * block, :] = coup_ref[0, a].T
    live = lax.broadcasted_iota(jnp.int32, (rows, modes), 0) < rows_ref[s]
    masked = jnp.where(live, modes_ref[0].astype(F32), 0.0).astype(BF16)
    reduced = jnp.dot(ct[...], masked, preferred_element_type=F32)
    rtb[...] = reduced.astype(BF16)
    wt[...] = (reduced * inv_ref[pl.ds(s, 1), :]).astype(BF16)
    row = lax.broadcasted_iota(jnp.int32, (half, block), 0)
    lane = lax.broadcasted_iota(jnp.int32, (half, block), 1)
    on_diagonal = lax.broadcasted_iota(jnp.int32, (block, block), 0) == (
        lax.broadcasted_iota(jnp.int32, (block, block), 1)
    )
    for a in range(links):
        own = slice(a * block, (a + 1) * block)
        contrib = lax.dot_general(
            wt[own, :], rtb[own, :], (((1,), (1,)), ((), ())), preferred_element_type=F32
        )
        lower = pltpu.roll(contrib[half:, :], half, 1)
        packed = jnp.where(row <= lane, contrib[:half, :], lower)
        diagonal = jnp.sum(jnp.where(on_diagonal, contrib, 0.0), axis=0, keepdims=True)
        ident = adj_ref[s, a]
        owner, b = ident // 256, ident % 16
        at = pl.ds(pl.multiple_of(b * half, half), half)
        out_ref[owner, at, :] = (out_ref[owner, at, :].astype(F32) + packed).astype(BF16)
        at = pl.ds(owner * 16 + b, 1)
        dg[at, :] = dg[at, :] + diagonal

    @pl.when(s == pl.num_programs(0) - 1)
    def _():
        for owner in range(8):
            out_ref[owner, 16 * half :, :] = dg[owner * 16 : owner * 16 + 16, :].astype(BF16)


def contributions(modes, coupling, inv_eig, sub_rows, adjacency):
    subs, rows, width = modes.shape
    links, block = coupling.shape[1], coupling.shape[3]
    return pl.pallas_call(
        contrib_kernel,
        out_shape=jax.ShapeDtypeStruct((8, PACKED, block), BF16),
        grid_spec=pltpu.PrefetchScalarGridSpec(
            num_scalar_prefetch=2,
            grid=(subs,),
            in_specs=[
                pl.BlockSpec((1, rows, width), lambda s, *_: (s, 0, 0)),
                pl.BlockSpec((1, links, rows, block), lambda s, *_: (s, 0, 0, 0)),
                pl.BlockSpec((subs, width), lambda s, *_: (0, 0)),
            ],
            out_specs=pl.BlockSpec((8, PACKED, block), lambda s, *_: (0, 0, 0)),
            scratch_shapes=[
                pltpu.VMEM((links * block, rows), BF16),
                pltpu.VMEM((links * block, width), BF16),
                pltpu.VMEM((links * block, width), BF16),
                pltpu.VMEM((128, block), F32),
            ],
        ),
        compiler_params=pltpu.CompilerParams(vmem_limit_bytes=67043328),
    )(sub_rows, adjacency, modes, coupling, inv_eig)


SCRATCH = {
    "dm": pltpu.VMEM((4, PACKED, 128), BF16),
    "rc": pltpu.VMEM((4, PACKED, 128), BF16),
    "mra": pltpu.VMEM((PACKED, 128), BF16),
    "mrb": pltpu.VMEM((2, PACKED, 128), BF16),
    "dgs": pltpu.VMEM((16, 128), F32),
    "base_v": pltpu.VMEM((16, 128, 128), F32),
    "mb": pltpu.VMEM((8, 256, 256), BF16),
    "psi_v": pltpu.VMEM((2048, 2048), BF16),
    "psit": pltpu.VMEM((2, 1024, 2048), BF16),
    "img": pltpu.VMEM((8, 2048, 256), BF16),
    "ps": pltpu.VMEM((8, 1024, 256), BF16),
    "rp": pltpu.VMEM((8, 1024, 256), BF16),
}
for part in range(2):
    for name in ("a", "b", "c", "ra"):
        SCRATCH[f"{name}{part}"] = pltpu.VMEM((4, 4, 128, 128), BF16)
    for name in ("cf", "q2"):
        SCRATCH[f"{name}{part}"] = pltpu.VMEM((4, 4, 128, 128), F32)
    SCRATCH[f"rb{part}"] = pltpu.VMEM((2, 4, 4, 128, 128), BF16)
    for name in ("sa", "sb", "sc", "sra"):
        SCRATCH[f"{name}{part}"] = pltpu.VMEM((4, 128, 128), BF16)
    SCRATCH[f"srb{part}"] = pltpu.VMEM((2, 4, 128, 128), BF16)
    SCRATCH[f"q3{part}"] = pltpu.VMEM((4, 128, 128), F32)
    SCRATCH[f"ta{part}"] = pltpu.VMEM((128, 128), F32)
    SCRATCH[f"tb{part}"] = pltpu.VMEM((2, 128, 128), F32)
MESSAGES = 128
SCRATCH["psem"] = pltpu.SemaphoreType.DMA((8,))
SCRATCH["lsem"] = pltpu.SemaphoreType.DMA((8,))
SCRATCH["ssem"] = pltpu.SemaphoreType.DMA((MESSAGES,))
SCRATCH["rsem"] = pltpu.SemaphoreType.DMA((MESSAGES,))


def project_kernel(d_ref, base_ref, psi_ref, out_ref, *scratch):
    v = dict(zip(SCRATCH, scratch))
    dm, rc, mra, mrb, mb, dgs = v["dm"], v["rc"], v["mra"], v["mrb"], v["mb"], v["dgs"]
    psi_v, psit, img, ps, rp = v["psi_v"], v["psit"], v["img"], v["ps"], v["rp"]
    ssem, rsem, lsem, psem = v["ssem"], v["rsem"], v["lsem"], v["psem"]

    def pair(name):
        return [v[f"{name}{p}"] for p in range(2)]

    pa, pb, pc, ra, cf, q2, rb = (pair(n) for n in ("a", "b", "c", "ra", "cf", "q2", "rb"))
    sa, sb, sc, sra, srb = (pair(n) for n in ("sa", "sb", "sc", "sra", "srb"))
    q3, ta, tb = (pair(n) for n in ("q3", "ta", "tb"))

    sub, tile = lax.axis_index("sub"), lax.axis_index("tile")
    core, x = lax.rem(sub, 2), lax.div(sub, 2)
    y, z = lax.div(tile, 4), lax.rem(tile, 4)
    partner = {"sub": x * 2 + 1 - core, "tile": tile}

    def step(axis, d):
        if axis == "x":
            return {"sub": lax.rem(x + d, 4) * 2 + core, "tile": tile}
        if axis == "y":
            return {"sub": sub, "tile": lax.rem(y + d, 4) * 4 + z}
        return {"sub": sub, "tile": y * 4 + lax.rem(z + d, 4)}

    plus = {a: step(a, 1) for a in "xyz"}
    minus = {a: step(a, 3) for a in "xyz"}

    barrier = pltpu.get_barrier_semaphore()
    peers = [partner] + [plus[a] for a in "xyz"] + [minus[a] for a in "xyz"]
    for peer in peers:
        pl.semaphore_signal(barrier, inc=1, device_id=peer, device_id_type=MESH)

    def psi_copy(k):
        rows = pl.ds(pl.multiple_of(k * 256, 256), 256)
        return pltpu.make_async_copy(psi_ref.at[rows], psi_v.at[rows], psem.at[k])

    own_d = []
    for i, d in enumerate(ORDER):
        at = lax.rem(x + d, 4) * 2 + core
        own_d.append(pltpu.make_async_copy(d_ref.at[at], dm.at[i], lsem.at[i]))
        own_d[-1].start()
    base_copy = pltpu.make_async_copy(base_ref, v["base_v"], lsem.at[4])

    pl.semaphore_wait(barrier, len(peers))

    count = [0]
    sent = []

    def message(src, dst, device):
        k = count[0]
        count[0] += 1
        copy = pltpu.make_async_remote_copy(
            src_ref=src,
            dst_ref=dst,
            send_sem=ssem.at[k],
            recv_sem=rsem.at[k],
            device_id=device,
            device_id_type=MESH,
        )
        copy.start()
        sent.append(copy)
        return copy

    from_core = []
    for i, d in enumerate(ORDER):
        at = lax.rem(x + d, 4) * 2 + 1 - core
        from_core.append(message(d_ref.at[at], rc.at[i], partner))
    for k in range(8):
        psi_copy(k).start()
    base_copy.start()

    def add_rows(dst, src, rows, chunk):
        @pl.loop(0, rows // chunk)
        def _(b):
            at = pl.ds(pl.multiple_of(b * chunk, 16), chunk)
            dst[at, :] = (dst[at, :].astype(F32) + src[at, :].astype(F32)).astype(BF16)

    def transpose_rows(first, last):
        @pl.loop(first, last)
        def _(k):
            psi_copy(k).wait()
            rows = pl.ds(pl.multiple_of(k * 256, 256), 256)
            for cc in range(2):
                for i, d in enumerate(ORDER):
                    band = lax.rem(x + d, 4) * 2 + (core if cc else 1 - core)
                    cols = pl.ds(pl.multiple_of(band * 256, 256), 256)
                    psit[cc, i * 256 : (i + 1) * 256, rows] = psi_v[rows, cols].T

    low, high = slice(0, 512), slice(512, PACKED)
    for i in range(4):
        own_d[i].wait()
        from_core[i].wait_recv()
        add_rows(dm.at[i], rc.at[i], PACKED, 80)
        if i == 0:
            m_ap = message(dm.at[0, low], mra.at[low], plus["x"])
            m_am = message(dm.at[0, high], mra.at[high], minus["x"])
        if i == 1:
            m_bp = message(dm.at[1, high], mrb.at[0, high], plus["x"])
        if i == 2:
            m_bm = message(dm.at[2, low], mrb.at[1, low], minus["x"])
    transpose_rows(0, 2)
    mb[...] = jnp.zeros(mb.shape, BF16)
    m_ap.wait_recv()
    add_rows(dm.at[1, low], mra.at[low], 512, 64)
    m_cp = message(dm.at[1, low], mrb.at[0, low], plus["x"])
    m_am.wait_recv()
    add_rows(dm.at[2, high], mra.at[high], PACKED - 512, 48)
    m_cm = message(dm.at[2, high], mrb.at[1, high], minus["x"])
    transpose_rows(2, 8)
    base_copy.wait()
    for m in (m_bp, m_bm, m_cp, m_cm):
        m.wait_recv()

    tail = slice(1024, PACKED)
    dgs[...] = dm[3, tail, :].astype(F32) + (
        mrb[0, tail, :].astype(F32) + mrb[1, tail, :].astype(F32)
    )
    row = lax.broadcasted_iota(jnp.int32, (64, 128), 0)
    lane = lax.broadcasted_iota(jnp.int32, (64, 128), 1)

    @pl.loop(0, 8)
    def _(j):
        for side in range(2):
            b = j * 2 + side
            at = pl.ds(pl.multiple_of(b * 64, 64), 64)
            packed = dm[3, at, :].astype(F32) + (
                mrb[0, at, :].astype(F32) + mrb[1, at, :].astype(F32)
            )
            turned = jnp.concatenate([packed, packed], axis=0).T
            top = jnp.where(row <= lane, packed, turned[:64])
            last = jnp.where(row + 64 < lane, turned[:64], dgs[pl.ds(b, 1), :])
            last = jnp.where(row + 64 > lane, pltpu.roll(packed, 64, 1), last)
            bottom = jnp.where(lane < 64, turned[64:], last)
            here = slice(side * 128, side * 128 + 64)
            cols = slice(side * 128, side * 128 + 128)
            mb[j, here, cols] = (top + v["base_v"][b, 0:64, :]).astype(BF16)
            here = slice(side * 128 + 64, side * 128 + 128)
            mb[j, here, cols] = (bottom + v["base_v"][b, 64:128, :]).astype(BF16)

    @pl.loop(0, 8)
    def _(j):
        rows = pl.ds(pl.multiple_of(j * 256, 256), 256)
        mass = mb[j]
        for u in range(8):
            iy, n = divmod(u, 2)
            tiles = []
            for t in range(2):
                at = lax.rem(y + ORDER[iy], 4) * 4 + lax.rem(z + ORDER[2 * n + t], 4)
                tiles.append(psi_v[rows, pl.ds(pl.multiple_of(at * 128, 128), 128)])
            rhs = jnp.concatenate(tiles, axis=1)
            img[u, rows, :] = jnp.dot(mass, rhs, preferred_element_type=F32).astype(BF16)

    half_base = count[0]
    count[0] += 8

    def half_copy(u):
        return pltpu.make_async_remote_copy(
            src_ref=ps.at[u],
            dst_ref=rp.at[u],
            send_sem=ssem.at[half_base + u],
            recv_sem=rsem.at[half_base + u],
            device_id=partner,
            device_id_type=MESH,
        )

    def other_half(u):
        ps[u] = jnp.dot(psit[0], img[u], preferred_element_type=F32).astype(BF16)
        half_copy(u).start()

    def own_half(iy, n):
        u = iy * 2 + n
        half_copy(u).wait_recv()
        acc = jnp.dot(psit[1], img[u], preferred_element_type=F32)
        acc = acc + rp[u].astype(F32)
        for ix in range(4):
            for t in range(2):
                iz = 2 * n + t
                cols = slice(t * 128, (t + 1) * 128)
                tile0 = acc[ix * 256 : ix * 256 + 128, cols]
                if ix == 0:
                    pa[0][iy, iz] = tile0.astype(BF16)
                elif ix == 3:
                    q2[0][iy, iz] = tile0
                elif (ix == 1) == (n == 0):
                    cf[0][iy, iz] = tile0
                else:
                    pb[0][iy, iz] = tile0.astype(BF16)
                tile1 = acc[ix * 256 + 128 : ix * 256 + 256, cols]
                if iz == 0:
                    pa[1][iy, ix] = tile1.astype(BF16)
                elif iz == 3:
                    q2[1][iy, ix] = tile1
                elif (iz == 1) == (ix < 2):
                    cf[1][iy, ix] = tile1
                else:
                    pb[1][iy, ix] = tile1.astype(BF16)

    way = (plus, minus)
    axes = (("x", "y", "z"), ("z", "y", "x"))
    first = {}
    halves = (slice(0, 2), slice(2, 4))

    def send_unmerged(iy, n):
        at = halves[n]
        first["a", 0, iy, n] = message(pa[0].at[iy, at], ra[0].at[iy, at], way[n]["x"])
        if n == 0:
            for side in range(2):
                at1 = halves[side]
                first["a", 1, iy, side] = message(
                    pa[1].at[iy, at1], ra[1].at[iy, at1], way[side]["z"]
                )
        side = 1 - n
        first["b", 0, iy, n] = message(pb[0].at[iy, at], rb[0].at[side, iy, at], way[side]["x"])
        at1 = halves[1 - n]
        first["b", 1, iy, n] = message(pb[1].at[iy, at1], rb[1].at[n, iy, at1], way[n]["z"])

    def send_merged(iy, n):
        at = halves[n]
        for p in range(2):
            first["a", p, iy, n].wait_recv()
            pc[p][iy, at] = (cf[p][iy, at] + ra[p][iy, at].astype(F32)).astype(BF16)
            first["c", p, iy, n] = message(
                pc[p].at[iy, at], rb[p].at[n, iy, at], way[n][axes[p][0]]
            )

    def finish_row(iy):
        for p in range(2):
            for n in range(2):
                first["b", p, iy, n].wait_recv()
                first["c", p, iy, n].wait_recv()
            q2[p][iy] = q2[p][iy] + (rb[p][0, iy].astype(F32) + rb[p][1, iy].astype(F32))

    second = {}

    def second_row(iy):
        finish_row(iy)
        for p in range(2):
            if iy == 0:
                sa[p][...] = q2[p][0].astype(BF16)
                for side in range(2):
                    at = halves[side]
                    second["a", p, side] = message(sa[p].at[at], sra[p].at[at], way[side]["y"])
            elif iy < 3:
                side = iy - 1
                at = halves[1 - side]
                sb[p][at] = q2[p][iy, at].astype(BF16)
                second["b", p, side] = message(sb[p].at[at], srb[p].at[side, at], way[side]["y"])
        if iy in (1, 2):
            for p in range(2):
                side = iy - 1
                at = halves[side]
                second["a", p, side].wait_recv()
                sc[p][at] = (q2[p][iy, at] + sra[p][at].astype(F32)).astype(BF16)
                second["c", p, side] = message(sc[p].at[at], srb[p].at[side, at], way[side]["y"])

    LAG = 3

    @pl.loop(0, LAG)
    def _(u):
        other_half(u)

    for u in range(8):
        iy, n = divmod(u, 2)
        own_half(iy, n)
        send_unmerged(iy, n)
        if 1 <= u <= 5:
            send_merged(*divmod(u - 1, 2))
        if u == 4:
            second_row(0)
        if u == 6:
            second_row(1)
        if u + LAG < 8:
            other_half(u + LAG)
    for u in (5, 6, 7):
        send_merged(*divmod(u, 2))
    second_row(2)
    second_row(3)

    for p in range(2):
        for side in range(2):
            second["b", p, side].wait_recv()
            second["c", p, side].wait_recv()
        q3[p][...] = q2[p][3] + (srb[p][0].astype(F32) + srb[p][1].astype(F32))

    third = {}
    cuts = (slice(0, 64), slice(64, 128))
    for p in range(2):
        axis = axes[p][2]
        for side in range(2):
            at, other = cuts[side], cuts[1 - side]
            third["a", p, side] = message(q3[p].at[0, at], ta[p].at[at], way[side][axis])
        for side in range(2):
            other = cuts[1 - side]
            third["b", p, side] = message(
                q3[p].at[1 + side, other], tb[p].at[side, other], way[side][axis]
            )
    for p in range(2):
        axis = axes[p][2]
        for side in range(2):
            at = cuts[side]
            third["a", p, side].wait_recv()
            q3[p][1 + side, at] = q3[p][1 + side, at] + ta[p][at]
            third["c", p, side] = message(
                q3[p].at[1 + side, at], tb[p].at[side, at], way[side][axis]
            )
    for p in range(2):
        for side in range(2):
            third["b", p, side].wait_recv()
            third["c", p, side].wait_recv()
        out_ref[p * 128 : (p + 1) * 128, :] = q3[p][3] + (tb[p][0] + tb[p][1])

    for copy in sent:
        copy.wait_send()

    @pl.loop(0, 8)
    def _(u):
        half_copy(u).wait_send()

    assert count[0] <= MESSAGES


def project(dense, base_mass, iface_modes):
    hbm = pl.BlockSpec(memory_space=pl.ANY)
    return pl.pallas_call(
        project_kernel,
        out_shape=jax.ShapeDtypeStruct((256, 128), F32),
        in_specs=[hbm, hbm, hbm],
        out_specs=pl.BlockSpec(memory_space=pltpu.VMEM),
        scratch_shapes=list(SCRATCH.values()),
        compiler_params=pltpu.CompilerParams(
            collective_id=0, has_side_effects=True, vmem_limit_bytes=67043328
        ),
    )(dense, base_mass, iface_modes)


def on_device(modes, coupling, inv_eig, sub_rows, adjacency, base_mass, iface_modes):
    dense = contributions(modes, coupling, inv_eig, sub_rows, adjacency)
    return project(dense, base_mass, iface_modes)


def solution(mesh):
    placed = (
        P(("sub", "tile"), None, None),
        P(("sub", "tile"), None, None, None),
        P(("sub", "tile"), None),
        P(("sub", "tile")),
        P(("sub", "tile"), None),
        P(("sub", "tile"), None, None),
        P(("sub", "tile"), None),
    )
    return jax.shard_map(
        on_device, mesh=mesh, in_specs=placed, out_specs=P("sub", "tile"), check_vma=False
    )
```

```python
import jax
import jax.numpy as jnp
from jax import lax
from jax.experimental import pallas as pl
from jax.experimental.pallas import tpu as pltpu
from jax.sharding import PartitionSpec as P

MESH = pl.DeviceIdType.MESH
F32 = jnp.float32
BF16 = jnp.bfloat16
ORDER = (2, 1, 3, 0)
TALL = (64, 96, 96)
START = (0, 64, 160)
PACKED = 16 * 64 + 16


def contrib_kernel(rows_ref, adj_ref, modes_ref, coup_ref, inv_ref, out_ref, ct, rtb, wt, dg):
    s = pl.program_id(0)
    links = coup_ref.shape[1]
    rows, modes = modes_ref.shape[1:]
    block = coup_ref.shape[3]
    half = block // 2

    @pl.when(s == 0)
    def _():
        dg[...] = jnp.zeros(dg.shape, F32)
        for owner in range(8):
            @pl.loop(0, PACKED // 80)
            def _(b):
                at = pl.ds(pl.multiple_of(b * 80, 16), 80)
                out_ref[owner, at, :] = jnp.zeros((80, block), BF16)

    for a in range(links):
        ct[a * block : (a + 1) * block, :] = coup_ref[0, a].T
    live = lax.broadcasted_iota(jnp.int32, (rows, modes), 0) < rows_ref[s]
    masked = jnp.where(live, modes_ref[0].astype(F32), 0.0).astype(BF16)
    reduced = jnp.dot(ct[...], masked, preferred_element_type=F32)
    rtb[...] = reduced.astype(BF16)
    wt[...] = (reduced * inv_ref[pl.ds(s, 1), :]).astype(BF16)
    row = lax.broadcasted_iota(jnp.int32, (half, block), 0)
    lane = lax.broadcasted_iota(jnp.int32, (half, block), 1)
    on_diagonal = lax.broadcasted_iota(jnp.int32, (block, block), 0) == (
        lax.broadcasted_iota(jnp.int32, (block, block), 1)
    )
    for a in range(links):
        own = slice(a * block, (a + 1) * block)
        contrib = lax.dot_general(
            wt[own, :], rtb[own, :], (((1,), (1,)), ((), ())), preferred_element_type=F32
        )
        lower = pltpu.roll(contrib[half:, :], half, 1)
        packed = jnp.where(row <= lane, contrib[:half, :], lower)
        diagonal = jnp.sum(jnp.where(on_diagonal, contrib, 0.0), axis=0, keepdims=True)
        ident = adj_ref[s, a]
        owner, b = ident // 256, ident % 16
        at = pl.ds(pl.multiple_of(b * half, half), half)
        out_ref[owner, at, :] = (out_ref[owner, at, :].astype(F32) + packed).astype(BF16)
        at = pl.ds(owner * 16 + b, 1)
        dg[at, :] = dg[at, :] + diagonal

    @pl.when(s == pl.num_programs(0) - 1)
    def _():
        for owner in range(8):
            out_ref[owner, 16 * half :, :] = dg[owner * 16 : owner * 16 + 16, :].astype(BF16)


def contributions(modes, coupling, inv_eig, sub_rows, adjacency):
    subs, rows, width = modes.shape
    links, block = coupling.shape[1], coupling.shape[3]
    return pl.pallas_call(
        contrib_kernel,
        out_shape=jax.ShapeDtypeStruct((8, PACKED, block), BF16),
        grid_spec=pltpu.PrefetchScalarGridSpec(
            num_scalar_prefetch=2,
            grid=(subs,),
            in_specs=[
                pl.BlockSpec((1, rows, width), lambda s, *_: (s, 0, 0)),
                pl.BlockSpec((1, links, rows, block), lambda s, *_: (s, 0, 0, 0)),
                pl.BlockSpec((subs, width), lambda s, *_: (0, 0)),
            ],
            out_specs=pl.BlockSpec((8, PACKED, block), lambda s, *_: (0, 0, 0)),
            scratch_shapes=[
                pltpu.VMEM((links * block, rows), BF16),
                pltpu.VMEM((links * block, width), BF16),
                pltpu.VMEM((links * block, width), BF16),
                pltpu.VMEM((128, block), F32),
            ],
        ),
        compiler_params=pltpu.CompilerParams(vmem_limit_bytes=67043328),
    )(sub_rows, adjacency, modes, coupling, inv_eig)


SCRATCH = {
    "dm": pltpu.VMEM((4, PACKED, 128), BF16),
    "rc": pltpu.VMEM((4, PACKED, 128), BF16),
    "mra": pltpu.VMEM((PACKED, 128), BF16),
    "mrb": pltpu.VMEM((2, PACKED, 128), BF16),
    "dgs": pltpu.VMEM((16, 128), F32),
    "base_v": pltpu.VMEM((16, 128, 128), F32),
    "mb": pltpu.VMEM((8, 256, 256), BF16),
    "psi_v": pltpu.VMEM((2048, 2048), BF16),
    "psit": pltpu.VMEM((2, 1024, 2048), BF16),
    "img": pltpu.VMEM((8, 2048, 256), BF16),
    "ps": pltpu.VMEM((8, 1024, 256), BF16),
    "rp": pltpu.VMEM((8, 1024, 256), BF16),
}
for part, tall in enumerate(TALL):
    for name in ("a", "b", "c", "ra"):
        SCRATCH[f"{name}{part}"] = pltpu.VMEM((4, 4, tall, 128), BF16)
    for name in ("cf", "q2"):
        SCRATCH[f"{name}{part}"] = pltpu.VMEM((4, 4, tall, 128), F32)
    SCRATCH[f"rb{part}"] = pltpu.VMEM((2, 4, 4, tall, 128), BF16)
    for name in ("sa", "sb", "sc", "sra"):
        SCRATCH[f"{name}{part}"] = pltpu.VMEM((4, tall, 128), BF16)
    SCRATCH[f"srb{part}"] = pltpu.VMEM((2, 4, tall, 128), BF16)
    SCRATCH[f"q3{part}"] = pltpu.VMEM((4, tall, 128), F32)
    SCRATCH[f"ta{part}"] = pltpu.VMEM((tall, 128), F32)
    SCRATCH[f"tb{part}"] = pltpu.VMEM((2, tall, 128), F32)
MESSAGES = 128
SCRATCH["psem"] = pltpu.SemaphoreType.DMA((8,))
SCRATCH["lsem"] = pltpu.SemaphoreType.DMA((8,))
SCRATCH["ssem"] = pltpu.SemaphoreType.DMA((MESSAGES,))
SCRATCH["rsem"] = pltpu.SemaphoreType.DMA((MESSAGES,))


def project_kernel(d_ref, base_ref, psi_ref, out_ref, *scratch):
    v = dict(zip(SCRATCH, scratch))
    dm, rc, mra, mrb, mb, dgs = v["dm"], v["rc"], v["mra"], v["mrb"], v["mb"], v["dgs"]
    psi_v, psit, img, ps, rp = v["psi_v"], v["psit"], v["img"], v["ps"], v["rp"]
    ssem, rsem, lsem, psem = v["ssem"], v["rsem"], v["lsem"], v["psem"]

    def pair(name):
        return [v[f"{name}{p}"] for p in range(3)]

    pa, pb, pc, ra, cf, q2, rb = (pair(n) for n in ("a", "b", "c", "ra", "cf", "q2", "rb"))
    sa, sb, sc, sra, srb = (pair(n) for n in ("sa", "sb", "sc", "sra", "srb"))
    q3, ta, tb = (pair(n) for n in ("q3", "ta", "tb"))

    sub, tile = lax.axis_index("sub"), lax.axis_index("tile")
    core, x = lax.rem(sub, 2), lax.div(sub, 2)
    y, z = lax.div(tile, 4), lax.rem(tile, 4)
    partner = {"sub": x * 2 + 1 - core, "tile": tile}

    def step(axis, d):
        if axis == "x":
            return {"sub": lax.rem(x + d, 4) * 2 + core, "tile": tile}
        if axis == "y":
            return {"sub": sub, "tile": lax.rem(y + d, 4) * 4 + z}
        return {"sub": sub, "tile": y * 4 + lax.rem(z + d, 4)}

    plus = {a: step(a, 1) for a in "xyz"}
    minus = {a: step(a, 3) for a in "xyz"}

    barrier = pltpu.get_barrier_semaphore()
    peers = [partner] + [plus[a] for a in "xyz"] + [minus[a] for a in "xyz"]
    for peer in peers:
        pl.semaphore_signal(barrier, inc=1, device_id=peer, device_id_type=MESH)

    def psi_copy(k):
        rows = pl.ds(pl.multiple_of(k * 256, 256), 256)
        return pltpu.make_async_copy(psi_ref.at[rows], psi_v.at[rows], psem.at[k])

    own_d = []
    for i, d in enumerate(ORDER):
        at = lax.rem(x + d, 4) * 2 + core
        own_d.append(pltpu.make_async_copy(d_ref.at[at], dm.at[i], lsem.at[i]))
        own_d[-1].start()
    base_copy = pltpu.make_async_copy(base_ref, v["base_v"], lsem.at[4])

    pl.semaphore_wait(barrier, len(peers))

    count = [0]
    sent = []

    def message(src, dst, device):
        k = count[0]
        count[0] += 1
        copy = pltpu.make_async_remote_copy(
            src_ref=src,
            dst_ref=dst,
            send_sem=ssem.at[k],
            recv_sem=rsem.at[k],
            device_id=device,
            device_id_type=MESH,
        )
        copy.start()
        sent.append(copy)
        return copy

    from_core = []
    for i, d in enumerate(ORDER):
        at = lax.rem(x + d, 4) * 2 + 1 - core
        from_core.append(message(d_ref.at[at], rc.at[i], partner))
    for k in range(8):
        psi_copy(k).start()
    base_copy.start()

    def add_rows(dst, src, rows, chunk):
        @pl.loop(0, rows // chunk)
        def _(b):
            at = pl.ds(pl.multiple_of(b * chunk, 16), chunk)
            dst[at, :] = (dst[at, :].astype(F32) + src[at, :].astype(F32)).astype(BF16)

    def transpose_rows(first, last):
        @pl.loop(first, last)
        def _(k):
            psi_copy(k).wait()
            rows = pl.ds(pl.multiple_of(k * 256, 256), 256)
            for cc in range(2):
                for i, d in enumerate(ORDER):
                    band = lax.rem(x + d, 4) * 2 + (core if cc else 1 - core)
                    cols = pl.ds(pl.multiple_of(band * 256, 256), 256)
                    psit[cc, i * 256 : (i + 1) * 256, rows] = psi_v[rows, cols].T

    low, high = slice(0, 512), slice(512, PACKED)
    for i in range(4):
        own_d[i].wait()
        from_core[i].wait_recv()
        add_rows(dm.at[i], rc.at[i], PACKED, 80)
        if i == 0:
            m_ap = message(dm.at[0, low], mra.at[low], plus["x"])
            m_am = message(dm.at[0, high], mra.at[high], minus["x"])
        if i == 1:
            m_bp = message(dm.at[1, high], mrb.at[0, high], plus["x"])
        if i == 2:
            m_bm = message(dm.at[2, low], mrb.at[1, low], minus["x"])
    transpose_rows(0, 2)
    mb[...] = jnp.zeros(mb.shape, BF16)
    m_ap.wait_recv()
    add_rows(dm.at[1, low], mra.at[low], 512, 64)
    m_cp = message(dm.at[1, low], mrb.at[0, low], plus["x"])
    m_am.wait_recv()
    add_rows(dm.at[2, high], mra.at[high], PACKED - 512, 48)
    m_cm = message(dm.at[2, high], mrb.at[1, high], minus["x"])
    transpose_rows(2, 8)
    base_copy.wait()
    for m in (m_bp, m_bm, m_cp, m_cm):
        m.wait_recv()

    tail = slice(1024, PACKED)
    dgs[...] = dm[3, tail, :].astype(F32) + (
        mrb[0, tail, :].astype(F32) + mrb[1, tail, :].astype(F32)
    )
    row = lax.broadcasted_iota(jnp.int32, (64, 128), 0)
    lane = lax.broadcasted_iota(jnp.int32, (64, 128), 1)

    @pl.loop(0, 8)
    def _(j):
        for side in range(2):
            b = j * 2 + side
            at = pl.ds(pl.multiple_of(b * 64, 64), 64)
            packed = dm[3, at, :].astype(F32) + (
                mrb[0, at, :].astype(F32) + mrb[1, at, :].astype(F32)
            )
            turned = jnp.concatenate([packed, packed], axis=0).T
            top = jnp.where(row <= lane, packed, turned[:64])
            last = jnp.where(row + 64 < lane, turned[:64], dgs[pl.ds(b, 1), :])
            last = jnp.where(row + 64 > lane, pltpu.roll(packed, 64, 1), last)
            bottom = jnp.where(lane < 64, turned[64:], last)
            here = slice(side * 128, side * 128 + 64)
            cols = slice(side * 128, side * 128 + 128)
            mb[j, here, cols] = (top + v["base_v"][b, 0:64, :]).astype(BF16)
            here = slice(side * 128 + 64, side * 128 + 128)
            mb[j, here, cols] = (bottom + v["base_v"][b, 64:128, :]).astype(BF16)

    @pl.loop(0, 8)
    def _(j):
        rows = pl.ds(pl.multiple_of(j * 256, 256), 256)
        mass = mb[j]
        for u in range(8):
            iy, n = divmod(u, 2)
            tiles = []
            for t in range(2):
                at = lax.rem(y + ORDER[iy], 4) * 4 + lax.rem(z + ORDER[2 * n + t], 4)
                tiles.append(psi_v[rows, pl.ds(pl.multiple_of(at * 128, 128), 128)])
            rhs = jnp.concatenate(tiles, axis=1)
            img[u, rows, :] = jnp.dot(mass, rhs, preferred_element_type=F32).astype(BF16)

    half_base = count[0]
    count[0] += 8

    def half_copy(u):
        return pltpu.make_async_remote_copy(
            src_ref=ps.at[u],
            dst_ref=rp.at[u],
            send_sem=ssem.at[half_base + u],
            recv_sem=rsem.at[half_base + u],
            device_id=partner,
            device_id_type=MESH,
        )

    def other_half(u):
        ps[u] = jnp.dot(psit[0], img[u], preferred_element_type=F32).astype(BF16)
        half_copy(u).start()

    def own_half(iy, n):
        u = iy * 2 + n
        half_copy(u).wait_recv()
        acc = jnp.dot(psit[1], img[u], preferred_element_type=F32)
        acc = acc + rp[u].astype(F32)
        for ix in range(4):
            for t in range(2):
                iz = 2 * n + t
                cols = slice(t * 128, (t + 1) * 128)
                tile = [
                    acc[ix * 256 + at : ix * 256 + at + tall, cols] for at, tall in zip(START, TALL)
                ]
                if iy == 0:
                    pa[0][iz, ix] = tile[0].astype(BF16)
                elif iy == 3:
                    q2[0][iz, ix] = tile[0]
                elif iy - 1 == n:
                    cf[0][iz, ix] = tile[0]
                else:
                    pb[0][iz, ix] = tile[0].astype(BF16)
                if ix == 0:
                    pa[1][iy, iz] = tile[1].astype(BF16)
                elif ix == 3:
                    q2[1][iy, iz] = tile[1]
                elif ix - 1 == n:
                    cf[1][iy, iz] = tile[1]
                else:
                    pb[1][iy, iz] = tile[1].astype(BF16)
                if iz == 0:
                    pa[2][iy, ix] = tile[2].astype(BF16)
                elif iz == 3:
                    q2[2][iy, ix] = tile[2]
                elif (iz == 1) == (ix < 2):
                    cf[2][iy, ix] = tile[2]
                else:
                    pb[2][iy, ix] = tile[2].astype(BF16)

    way = (plus, minus)
    axes = (("y", "z", "x"), ("x", "y", "z"), ("z", "y", "x"))
    first = {}
    halves = (slice(0, 2), slice(2, 4))

    def send_unmerged(iy, n):
        at, other = halves[n], halves[1 - n]
        side = 1 - n
        if iy == 0:
            first["a", 0, n] = message(pa[0].at[at], ra[0].at[at], way[n]["y"])
        elif iy < 3 and iy - 1 != n:
            first["b", 0, n] = message(pb[0].at[at], rb[0].at[iy - 1, at], way[iy - 1]["y"])
        first["a", 1, iy, n] = message(pa[1].at[iy, at], ra[1].at[iy, at], way[n]["x"])
        if n == 0:
            for k in range(2):
                part = halves[k]
                first["a", 2, iy, k] = message(
                    pa[2].at[iy, part], ra[2].at[iy, part], way[k]["z"]
                )
        first["b", 1, iy, n] = message(pb[1].at[iy, at], rb[1].at[side, iy, at], way[side]["x"])
        first["b", 2, iy, n] = message(pb[2].at[iy, other], rb[2].at[n, iy, other], way[n]["z"])
        if iy - 1 == n:
            first["a", 0, n].wait_recv()
            pc[0][at] = (cf[0][at] + ra[0][at].astype(F32)).astype(BF16)
            first["c", 0, n] = message(pc[0].at[at], rb[0].at[n, at], way[n]["y"])

    def send_merged(u):
        iy, n = divmod(u, 2)
        at = halves[n]
        for p in (1, 2):
            first["a", p, iy, n].wait_recv()
            pc[p][iy, at] = (cf[p][iy, at] + ra[p][iy, at].astype(F32)).astype(BF16)
            first["c", p, iy, n] = message(
                pc[p].at[iy, at], rb[p].at[n, iy, at], way[n][axes[p][0]]
            )

    def finish_row(iy):
        for p in (1, 2):
            for n in range(2):
                first["b", p, iy, n].wait_recv()
                first["c", p, iy, n].wait_recv()
            q2[p][iy] = q2[p][iy] + (rb[p][0, iy].astype(F32) + rb[p][1, iy].astype(F32))

    second = {}

    def second_far(p):
        sa[p][...] = q2[p][0].astype(BF16)
        for side in range(2):
            at = halves[side]
            second["a", p, side] = message(
                sa[p].at[at], sra[p].at[at], way[side][axes[p][1]]
            )

    def second_unmerged(p, side):
        at = halves[1 - side]
        sb[p][at] = q2[p][1 + side, at].astype(BF16)
        second["b", p, side] = message(sb[p].at[at], srb[p].at[side, at], way[side][axes[p][1]])

    def second_merged(p, side):
        at = halves[side]
        second["a", p, side].wait_recv()
        sc[p][at] = (q2[p][1 + side, at] + sra[p][at].astype(F32)).astype(BF16)
        second["c", p, side] = message(sc[p].at[at], srb[p].at[side, at], way[side][axes[p][1]])

    def second_row(iy):
        finish_row(iy)
        for p in (1, 2):
            if iy == 0:
                second_far(p)
            elif iy < 3:
                second_unmerged(p, iy - 1)
        if iy in (1, 2):
            for p in (1, 2):
                second_merged(p, iy - 1)

    third = {}

    def third_send(p):
        for side in range(2):
            second["b", p, side].wait_recv()
            second["c", p, side].wait_recv()
        q3[p][...] = q2[p][3] + (srb[p][0].astype(F32) + srb[p][1].astype(F32))
        axis, cut = axes[p][2], TALL[p] // 2
        cuts = (slice(0, cut), slice(cut, 2 * cut))
        for side in range(2):
            at = cuts[side]
            third["a", p, side] = message(q3[p].at[0, at], ta[p].at[at], way[side][axis])
        for side in range(2):
            at = cuts[1 - side]
            third["b", p, side] = message(
                q3[p].at[1 + side, at], tb[p].at[side, at], way[side][axis]
            )

    def third_merge(p):
        axis, cut = axes[p][2], TALL[p] // 2
        cuts = (slice(0, cut), slice(cut, 2 * cut))
        for side in range(2):
            at = cuts[side]
            third["a", p, side].wait_recv()
            q3[p][1 + side, at] = q3[p][1 + side, at] + ta[p][at]
            third["c", p, side] = message(
                q3[p].at[1 + side, at], tb[p].at[side, at], way[side][axis]
            )

    def third_finish(p):
        for side in range(2):
            third["b", p, side].wait_recv()
            third["c", p, side].wait_recv()
        out_ref[START[p] : START[p] + TALL[p], :] = q3[p][3] + (tb[p][0] + tb[p][1])

    def own_piece(u):
        own_half(*divmod(u, 2))
        send_unmerged(*divmod(u, 2))

    def other_pieces(first_piece, last_piece):
        @pl.loop(first_piece, last_piece)
        def _(u):
            other_half(u)

    other_pieces(0, 2)
    own_half(*divmod(0, 2))
    other_pieces(2, 3)
    send_unmerged(*divmod(0, 2))
    own_half(*divmod(1, 2))
    other_pieces(3, 4)
    send_unmerged(*divmod(1, 2))
    own_half(*divmod(2, 2))
    other_pieces(4, 5)
    send_unmerged(*divmod(2, 2))
    send_merged(0)
    own_half(*divmod(3, 2))
    other_pieces(5, 6)
    send_unmerged(*divmod(3, 2))
    send_merged(1)
    own_half(*divmod(4, 2))
    other_pieces(6, 7)
    send_unmerged(*divmod(4, 2))
    send_merged(2)
    own_half(*divmod(5, 2))
    other_pieces(7, 8)
    send_unmerged(*divmod(5, 2))
    send_merged(3)
    own_half(*divmod(6, 2))
    send_unmerged(*divmod(6, 2))
    send_merged(4)
    second_row(0)
    own_half(*divmod(7, 2))
    send_unmerged(*divmod(7, 2))
    send_merged(5)
    second_row(1)
    send_merged(6)
    for side in range(2):
        first["b", 0, 1 - side].wait_recv()
        first["c", 0, side].wait_recv()
    q2[0][...] = q2[0][...] + (rb[0][0].astype(F32) + rb[0][1].astype(F32))
    second_far(0)
    for side in range(2):
        second_unmerged(0, side)
    send_merged(7)
    second_row(2)
    for side in range(2):
        second_merged(0, side)
    finish_row(3)
    for p in (1, 2, 0):
        third_send(p)
    for p in (1, 2, 0):
        third_merge(p)
    for p in (1, 2, 0):
        third_finish(p)

    for copy in sent:
        copy.wait_send()

    @pl.loop(0, 8)
    def _(u):
        half_copy(u).wait_send()

    assert count[0] <= MESSAGES


def project(dense, base_mass, iface_modes):
    hbm = pl.BlockSpec(memory_space=pl.ANY)
    return pl.pallas_call(
        project_kernel,
        out_shape=jax.ShapeDtypeStruct((256, 128), F32),
        in_specs=[hbm, hbm, hbm],
        out_specs=pl.BlockSpec(memory_space=pltpu.VMEM),
        scratch_shapes=list(SCRATCH.values()),
        compiler_params=pltpu.CompilerParams(
            collective_id=0, has_side_effects=True, vmem_limit_bytes=67043328
        ),
    )(dense, base_mass, iface_modes)


def on_device(modes, coupling, inv_eig, sub_rows, adjacency, base_mass, iface_modes):
    dense = contributions(modes, coupling, inv_eig, sub_rows, adjacency)
    return project(dense, base_mass, iface_modes)


def solution(mesh):
    placed = (
        P(("sub", "tile"), None, None),
        P(("sub", "tile"), None, None, None),
        P(("sub", "tile"), None),
        P(("sub", "tile")),
        P(("sub", "tile"), None),
        P(("sub", "tile"), None, None),
        P(("sub", "tile"), None),
    )
    return jax.shard_map(
        on_device, mesh=mesh, in_specs=placed, out_specs=P("sub", "tile"), check_vma=False
    )
```

```python
import jax
import jax.numpy as jnp
from jax import lax
from jax.experimental import pallas as pl
from jax.experimental.pallas import tpu as pltpu
from jax.sharding import PartitionSpec as P

MESH = pl.DeviceIdType.MESH
F32 = jnp.float32
BF16 = jnp.bfloat16
ORDER = (2, 1, 3, 0)
TALL = (64, 96, 96)
START = (0, 64, 160)
PACKED = 16 * 64 + 16


def contrib_kernel(
    rows_ref, adj_ref, inv_ref, modes_ref, coup_ref, out_ref, modes_v, coup_v, sems, ct, rtb, wt, dg
):
    subs, links = coup_ref.shape[:2]
    rows, modes = modes_ref.shape[1:]
    block = coup_ref.shape[3]
    half = block // 2

    def copies(s):
        yield pltpu.make_async_copy(modes_ref.at[s], modes_v.at[s], sems.at[s, 0])
        for k in range(2):
            part = pl.ds(k * (links // 2), links // 2)
            yield pltpu.make_async_copy(
                coup_ref.at[s, part], coup_v.at[s, part], sems.at[s, 1 + k]
            )

    for s in range(subs):
        for copy in copies(s):
            copy.start()
    dg[...] = jnp.zeros(dg.shape, F32)
    for owner in range(8):
        @pl.loop(0, PACKED // 80)
        def _(b):
            at = pl.ds(pl.multiple_of(b * 80, 16), 80)
            out_ref[owner, at, :] = jnp.zeros((80, block), BF16)

    @pl.loop(0, subs)
    def _(s):
        for copy in copies(s):
            copy.wait()
        one_substructure(
            s, rows_ref, adj_ref, inv_ref, modes_v, coup_v, out_ref, ct, rtb, wt, dg
        )

    for owner in range(8):
        out_ref[owner, 16 * half :, :] = dg[owner * 16 : owner * 16 + 16, :].astype(BF16)


def one_substructure(s, rows_ref, adj_ref, inv_ref, modes_v, coup_v, out_ref, ct, rtb, wt, dg):
    links = coup_v.shape[1]
    rows, modes = modes_v.shape[1:]
    block = coup_v.shape[3]
    half = block // 2
    for a in range(links):
        ct[a * block : (a + 1) * block, :] = coup_v[s, a].T
    live = lax.broadcasted_iota(jnp.int32, (rows, modes), 0) < rows_ref[s]
    masked = jnp.where(live, modes_v[s].astype(F32), 0.0).astype(BF16)
    reduced = jnp.dot(ct[...], masked, preferred_element_type=F32)
    rtb[...] = reduced.astype(BF16)
    wt[...] = (reduced * inv_ref[pl.ds(s, 1), :]).astype(BF16)
    row = lax.broadcasted_iota(jnp.int32, (half, block), 0)
    lane = lax.broadcasted_iota(jnp.int32, (half, block), 1)
    on_diagonal = lax.broadcasted_iota(jnp.int32, (block, block), 0) == (
        lax.broadcasted_iota(jnp.int32, (block, block), 1)
    )
    for a in range(links):
        own = slice(a * block, (a + 1) * block)
        contrib = lax.dot_general(
            wt[own, :], rtb[own, :], (((1,), (1,)), ((), ())), preferred_element_type=F32
        )
        lower = pltpu.roll(contrib[half:, :], half, 1)
        packed = jnp.where(row <= lane, contrib[:half, :], lower)
        diagonal = jnp.sum(jnp.where(on_diagonal, contrib, 0.0), axis=0, keepdims=True)
        ident = adj_ref[s, a]
        owner, b = ident // 256, ident % 16
        at = pl.ds(pl.multiple_of(b * half, half), half)
        out_ref[owner, at, :] = (out_ref[owner, at, :].astype(F32) + packed).astype(BF16)
        at = pl.ds(owner * 16 + b, 1)
        dg[at, :] = dg[at, :] + diagonal


def contributions(modes, coupling, inv_eig, sub_rows, adjacency):
    subs, rows, width = modes.shape
    links, block = coupling.shape[1], coupling.shape[3]
    return pl.pallas_call(
        contrib_kernel,
        out_shape=jax.ShapeDtypeStruct((8, PACKED, block), BF16),
        in_specs=[
            pl.BlockSpec(memory_space=pltpu.SMEM),
            pl.BlockSpec(memory_space=pltpu.SMEM),
            pl.BlockSpec(memory_space=pltpu.VMEM),
            pl.BlockSpec(memory_space=pl.ANY),
            pl.BlockSpec(memory_space=pl.ANY),
        ],
        out_specs=pl.BlockSpec(memory_space=pltpu.VMEM),
        scratch_shapes=[
            pltpu.VMEM((subs, rows, width), BF16),
            pltpu.VMEM((subs, links, rows, block), BF16),
            pltpu.SemaphoreType.DMA((subs, 3)),
            pltpu.VMEM((links * block, rows), BF16),
            pltpu.VMEM((links * block, width), BF16),
            pltpu.VMEM((links * block, width), BF16),
            pltpu.VMEM((128, block), F32),
        ],
        compiler_params=pltpu.CompilerParams(vmem_limit_bytes=67043328),
    )(sub_rows, adjacency, inv_eig, modes, coupling)


SCRATCH = {
    "dm": pltpu.VMEM((4, PACKED, 128), BF16),
    "rc": pltpu.VMEM((4, PACKED, 128), BF16),
    "mra": pltpu.VMEM((PACKED, 128), BF16),
    "mrb": pltpu.VMEM((2, PACKED, 128), BF16),
    "dgs": pltpu.VMEM((16, 128), F32),
    "base_v": pltpu.VMEM((16, 128, 128), F32),
    "mb": pltpu.VMEM((8, 256, 256), BF16),
    "psi_v": pltpu.VMEM((2048, 2048), BF16),
    "psit": pltpu.VMEM((2, 1024, 2048), BF16),
    "img": pltpu.VMEM((8, 2048, 256), BF16),
    "ps": pltpu.VMEM((8, 1024, 256), BF16),
    "rp": pltpu.VMEM((8, 1024, 256), BF16),
}
for part, tall in enumerate(TALL):
    for name in ("a", "b", "c", "ra"):
        SCRATCH[f"{name}{part}"] = pltpu.VMEM((4, 4, tall, 128), BF16)
    for name in ("cf", "q2"):
        SCRATCH[f"{name}{part}"] = pltpu.VMEM((4, 4, tall, 128), F32)
    SCRATCH[f"rb{part}"] = pltpu.VMEM((2, 4, 4, tall, 128), BF16)
    for name in ("sa", "sb", "sc", "sra"):
        SCRATCH[f"{name}{part}"] = pltpu.VMEM((4, tall, 128), BF16)
    SCRATCH[f"srb{part}"] = pltpu.VMEM((2, 4, tall, 128), BF16)
    SCRATCH[f"q3{part}"] = pltpu.VMEM((4, tall, 128), F32)
    SCRATCH[f"ta{part}"] = pltpu.VMEM((tall, 128), F32)
    SCRATCH[f"tb{part}"] = pltpu.VMEM((2, tall, 128), F32)
MESSAGES = 128
SCRATCH["psem"] = pltpu.SemaphoreType.DMA((8,))
SCRATCH["lsem"] = pltpu.SemaphoreType.DMA((8,))
SCRATCH["ssem"] = pltpu.SemaphoreType.DMA((MESSAGES,))
SCRATCH["rsem"] = pltpu.SemaphoreType.DMA((MESSAGES,))


def project_kernel(d_ref, base_ref, psi_ref, out_ref, *scratch):
    v = dict(zip(SCRATCH, scratch))
    dm, rc, mra, mrb, mb, dgs = v["dm"], v["rc"], v["mra"], v["mrb"], v["mb"], v["dgs"]
    psi_v, psit, img, ps, rp = v["psi_v"], v["psit"], v["img"], v["ps"], v["rp"]
    ssem, rsem, lsem, psem = v["ssem"], v["rsem"], v["lsem"], v["psem"]

    def pair(name):
        return [v[f"{name}{p}"] for p in range(3)]

    pa, pb, pc, ra, cf, q2, rb = (pair(n) for n in ("a", "b", "c", "ra", "cf", "q2", "rb"))
    sa, sb, sc, sra, srb = (pair(n) for n in ("sa", "sb", "sc", "sra", "srb"))
    q3, ta, tb = (pair(n) for n in ("q3", "ta", "tb"))

    sub, tile = lax.axis_index("sub"), lax.axis_index("tile")
    core, x = lax.rem(sub, 2), lax.div(sub, 2)
    y, z = lax.div(tile, 4), lax.rem(tile, 4)
    partner = {"sub": x * 2 + 1 - core, "tile": tile}

    def step(axis, d):
        if axis == "x":
            return {"sub": lax.rem(x + d, 4) * 2 + core, "tile": tile}
        if axis == "y":
            return {"sub": sub, "tile": lax.rem(y + d, 4) * 4 + z}
        return {"sub": sub, "tile": y * 4 + lax.rem(z + d, 4)}

    plus = {a: step(a, 1) for a in "xyz"}
    minus = {a: step(a, 3) for a in "xyz"}

    barrier = pltpu.get_barrier_semaphore()
    peers = [partner] + [plus[a] for a in "xyz"] + [minus[a] for a in "xyz"]
    for peer in peers:
        pl.semaphore_signal(barrier, inc=1, device_id=peer, device_id_type=MESH)

    def psi_copy(k):
        rows = pl.ds(pl.multiple_of(k * 256, 256), 256)
        return pltpu.make_async_copy(psi_ref.at[rows], psi_v.at[rows], psem.at[k])

    own_d = []
    for i, d in enumerate(ORDER):
        at = lax.rem(x + d, 4) * 2 + core
        own_d.append(pltpu.make_async_copy(d_ref.at[at], dm.at[i], lsem.at[i]))
        own_d[-1].start()
    base_copy = pltpu.make_async_copy(base_ref, v["base_v"], lsem.at[4])

    pl.semaphore_wait(barrier, len(peers))

    count = [0]
    sent = []

    def message(src, dst, device):
        k = count[0]
        count[0] += 1
        copy = pltpu.make_async_remote_copy(
            src_ref=src,
            dst_ref=dst,
            send_sem=ssem.at[k],
            recv_sem=rsem.at[k],
            device_id=device,
            device_id_type=MESH,
        )
        copy.start()
        sent.append(copy)
        return copy

    from_core = []
    for i, d in enumerate(ORDER):
        at = lax.rem(x + d, 4) * 2 + 1 - core
        from_core.append(message(d_ref.at[at], rc.at[i], partner))
    for k in range(8):
        psi_copy(k).start()
    base_copy.start()

    def add_rows(dst, src, rows, chunk):
        for b in range(0, rows, chunk):
            at = slice(b, b + chunk)
            dst[at, :] = (dst[at, :].astype(F32) + src[at, :].astype(F32)).astype(BF16)

    def transpose_rows(first, last):
        @pl.loop(first, last)
        def _(k):
            psi_copy(k).wait()
            rows = pl.ds(pl.multiple_of(k * 256, 256), 256)
            for cc in range(2):
                for i, d in enumerate(ORDER):
                    band = lax.rem(x + d, 4) * 2 + (core if cc else 1 - core)
                    cols = pl.ds(pl.multiple_of(band * 256, 256), 256)
                    psit[cc, i * 256 : (i + 1) * 256, rows] = psi_v[rows, cols].T

    low, high = slice(0, 512), slice(512, PACKED)
    for i in range(4):
        own_d[i].wait()
        from_core[i].wait_recv()
        add_rows(dm.at[i], rc.at[i], PACKED, 80)
        if i == 0:
            m_ap = message(dm.at[0, low], mra.at[low], plus["x"])
            m_am = message(dm.at[0, high], mra.at[high], minus["x"])
        if i == 1:
            m_bp = message(dm.at[1, high], mrb.at[0, high], plus["x"])
        if i == 2:
            m_bm = message(dm.at[2, low], mrb.at[1, low], minus["x"])
    transpose_rows(0, 2)
    mb[...] = jnp.zeros(mb.shape, BF16)
    m_ap.wait_recv()
    add_rows(dm.at[1, low], mra.at[low], 512, 64)
    m_cp = message(dm.at[1, low], mrb.at[0, low], plus["x"])
    m_am.wait_recv()
    add_rows(dm.at[2, high], mra.at[high], PACKED - 512, 48)
    m_cm = message(dm.at[2, high], mrb.at[1, high], minus["x"])
    transpose_rows(2, 8)
    base_copy.wait()
    for m in (m_bp, m_bm, m_cp, m_cm):
        m.wait_recv()

    tail = slice(1024, PACKED)
    dgs[...] = dm[3, tail, :].astype(F32) + (
        mrb[0, tail, :].astype(F32) + mrb[1, tail, :].astype(F32)
    )
    row = lax.broadcasted_iota(jnp.int32, (64, 128), 0)
    lane = lax.broadcasted_iota(jnp.int32, (64, 128), 1)

    @pl.loop(0, 8, unroll=2)
    def _(j):
        for side in range(2):
            b = j * 2 + side
            at = pl.ds(pl.multiple_of(b * 64, 64), 64)
            packed = dm[3, at, :].astype(F32) + (
                mrb[0, at, :].astype(F32) + mrb[1, at, :].astype(F32)
            )
            turned = jnp.concatenate([packed, packed], axis=0).T
            top = jnp.where(row <= lane, packed, turned[:64])
            last = jnp.where(row + 64 < lane, turned[:64], dgs[pl.ds(b, 1), :])
            last = jnp.where(row + 64 > lane, pltpu.roll(packed, 64, 1), last)
            bottom = jnp.where(lane < 64, turned[64:], last)
            here = slice(side * 128, side * 128 + 64)
            cols = slice(side * 128, side * 128 + 128)
            mb[j, here, cols] = (top + v["base_v"][b, 0:64, :]).astype(BF16)
            here = slice(side * 128 + 64, side * 128 + 128)
            mb[j, here, cols] = (bottom + v["base_v"][b, 64:128, :]).astype(BF16)

    @pl.loop(0, 8)
    def _(j):
        rows = pl.ds(pl.multiple_of(j * 256, 256), 256)
        mass = mb[j]
        for u in range(8):
            iy, n = divmod(u, 2)
            tiles = []
            for t in range(2):
                at = lax.rem(y + ORDER[iy], 4) * 4 + lax.rem(z + ORDER[2 * n + t], 4)
                tiles.append(psi_v[rows, pl.ds(pl.multiple_of(at * 128, 128), 128)])
            rhs = jnp.concatenate(tiles, axis=1)
            img[u, rows, :] = jnp.dot(mass, rhs, preferred_element_type=F32).astype(BF16)

    half_base = count[0]
    count[0] += 8

    def half_copy(u):
        return pltpu.make_async_remote_copy(
            src_ref=ps.at[u],
            dst_ref=rp.at[u],
            send_sem=ssem.at[half_base + u],
            recv_sem=rsem.at[half_base + u],
            device_id=partner,
            device_id_type=MESH,
        )

    def other_half(u):
        ps[u] = jnp.dot(psit[0], img[u], preferred_element_type=F32).astype(BF16)
        half_copy(u).start()

    def own_half(iy, n):
        u = iy * 2 + n
        half_copy(u).wait_recv()
        acc = jnp.dot(psit[1], img[u], preferred_element_type=F32)
        acc = acc + rp[u].astype(F32)
        for ix in range(4):
            for t in range(2):
                iz = 2 * n + t
                cols = slice(t * 128, (t + 1) * 128)
                tile = [
                    acc[ix * 256 + at : ix * 256 + at + tall, cols] for at, tall in zip(START, TALL)
                ]
                if iy == 0:
                    pa[0][iz, ix] = tile[0].astype(BF16)
                elif iy == 3:
                    q2[0][iz, ix] = tile[0]
                elif iy - 1 == n:
                    cf[0][iz, ix] = tile[0]
                else:
                    pb[0][iz, ix] = tile[0].astype(BF16)
                if ix == 0:
                    pa[1][iy, iz] = tile[1].astype(BF16)
                elif ix == 3:
                    q2[1][iy, iz] = tile[1]
                elif ix - 1 == n:
                    cf[1][iy, iz] = tile[1]
                else:
                    pb[1][iy, iz] = tile[1].astype(BF16)
                if iz == 0:
                    pa[2][iy, ix] = tile[2].astype(BF16)
                elif iz == 3:
                    q2[2][iy, ix] = tile[2]
                elif (iz == 1) == (ix < 2):
                    cf[2][iy, ix] = tile[2]
                else:
                    pb[2][iy, ix] = tile[2].astype(BF16)

    way = (plus, minus)
    axes = (("y", "z", "x"), ("x", "y", "z"), ("z", "y", "x"))
    first = {}
    halves = (slice(0, 2), slice(2, 4))

    def send_unmerged(iy, n):
        at, other = halves[n], halves[1 - n]
        side = 1 - n
        if iy == 0:
            first["a", 0, n] = message(pa[0].at[at], ra[0].at[at], way[n]["y"])
        elif iy < 3 and iy - 1 != n:
            first["b", 0, n] = message(pb[0].at[at], rb[0].at[iy - 1, at], way[iy - 1]["y"])
        first["a", 1, iy, n] = message(pa[1].at[iy, at], ra[1].at[iy, at], way[n]["x"])
        if n == 0:
            for k in range(2):
                part = halves[k]
                first["a", 2, iy, k] = message(
                    pa[2].at[iy, part], ra[2].at[iy, part], way[k]["z"]
                )
        first["b", 1, iy, n] = message(pb[1].at[iy, at], rb[1].at[side, iy, at], way[side]["x"])
        first["b", 2, iy, n] = message(pb[2].at[iy, other], rb[2].at[n, iy, other], way[n]["z"])
        if iy - 1 == n:
            first["a", 0, n].wait_recv()
            pc[0][at] = (cf[0][at] + ra[0][at].astype(F32)).astype(BF16)
            first["c", 0, n] = message(pc[0].at[at], rb[0].at[n, at], way[n]["y"])

    def send_merged(u):
        iy, n = divmod(u, 2)
        at = halves[n]
        for p in (1, 2):
            first["a", p, iy, n].wait_recv()
            pc[p][iy, at] = (cf[p][iy, at] + ra[p][iy, at].astype(F32)).astype(BF16)
            first["c", p, iy, n] = message(
                pc[p].at[iy, at], rb[p].at[n, iy, at], way[n][axes[p][0]]
            )

    def finish_row(iy):
        for p in (1, 2):
            for n in range(2):
                first["b", p, iy, n].wait_recv()
                first["c", p, iy, n].wait_recv()
            q2[p][iy] = q2[p][iy] + (rb[p][0, iy].astype(F32) + rb[p][1, iy].astype(F32))

    second = {}

    def second_far(p):
        sa[p][...] = q2[p][0].astype(BF16)
        for side in range(2):
            at = halves[side]
            second["a", p, side] = message(
                sa[p].at[at], sra[p].at[at], way[side][axes[p][1]]
            )

    def second_unmerged(p, side):
        at = halves[1 - side]
        sb[p][at] = q2[p][1 + side, at].astype(BF16)
        second["b", p, side] = message(sb[p].at[at], srb[p].at[side, at], way[side][axes[p][1]])

    def second_merged(p, side):
        at = halves[side]
        second["a", p, side].wait_recv()
        sc[p][at] = (q2[p][1 + side, at] + sra[p][at].astype(F32)).astype(BF16)
        second["c", p, side] = message(sc[p].at[at], srb[p].at[side, at], way[side][axes[p][1]])

    def second_row(iy):
        finish_row(iy)
        for p in (1, 2):
            if iy == 0:
                second_far(p)
            elif iy < 3:
                second_unmerged(p, iy - 1)
        if iy in (1, 2):
            for p in (1, 2):
                second_merged(p, iy - 1)

    third = {}

    def third_send(p):
        for side in range(2):
            second["b", p, side].wait_recv()
            second["c", p, side].wait_recv()
        q3[p][...] = q2[p][3] + (srb[p][0].astype(F32) + srb[p][1].astype(F32))
        axis, cut = axes[p][2], TALL[p] // 2
        cuts = (slice(0, cut), slice(cut, 2 * cut))
        for side in range(2):
            at = cuts[side]
            third["a", p, side] = message(q3[p].at[0, at], ta[p].at[at], way[side][axis])
        for side in range(2):
            at = cuts[1 - side]
            third["b", p, side] = message(
                q3[p].at[1 + side, at], tb[p].at[side, at], way[side][axis]
            )

    def third_merge(p):
        axis, cut = axes[p][2], TALL[p] // 2
        cuts = (slice(0, cut), slice(cut, 2 * cut))
        for side in range(2):
            at = cuts[side]
            third["a", p, side].wait_recv()
            q3[p][1 + side, at] = q3[p][1 + side, at] + ta[p][at]
            third["c", p, side] = message(
                q3[p].at[1 + side, at], tb[p].at[side, at], way[side][axis]
            )

    def third_finish(p):
        for side in range(2):
            third["b", p, side].wait_recv()
            third["c", p, side].wait_recv()
        out_ref[START[p] : START[p] + TALL[p], :] = q3[p][3] + (tb[p][0] + tb[p][1])

    def own_piece(u):
        own_half(*divmod(u, 2))
        send_unmerged(*divmod(u, 2))

    def other_pieces(first_piece, last_piece):
        @pl.loop(first_piece, last_piece)
        def _(u):
            other_half(u)

    other_pieces(0, 2)
    own_half(*divmod(0, 2))
    other_pieces(2, 3)
    send_unmerged(*divmod(0, 2))
    own_half(*divmod(1, 2))
    other_pieces(3, 4)
    send_unmerged(*divmod(1, 2))
    own_half(*divmod(2, 2))
    other_pieces(4, 5)
    send_unmerged(*divmod(2, 2))
    send_merged(0)
    own_half(*divmod(3, 2))
    other_pieces(5, 6)
    send_unmerged(*divmod(3, 2))
    send_merged(1)
    own_half(*divmod(4, 2))
    other_pieces(6, 7)
    send_unmerged(*divmod(4, 2))
    send_merged(2)
    own_half(*divmod(5, 2))
    other_pieces(7, 8)
    send_unmerged(*divmod(5, 2))
    send_merged(3)
    own_half(*divmod(6, 2))
    send_unmerged(*divmod(6, 2))
    send_merged(4)
    second_row(0)
    own_half(*divmod(7, 2))
    send_unmerged(*divmod(7, 2))
    send_merged(5)
    second_row(1)
    send_merged(6)
    for side in range(2):
        first["b", 0, 1 - side].wait_recv()
        first["c", 0, side].wait_recv()
    q2[0][...] = q2[0][...] + (rb[0][0].astype(F32) + rb[0][1].astype(F32))
    second_far(0)
    for side in range(2):
        second_unmerged(0, side)
    send_merged(7)
    second_row(2)
    for side in range(2):
        second_merged(0, side)
    finish_row(3)
    for p in (1, 2, 0):
        third_send(p)
    for p in (1, 2, 0):
        third_merge(p)
    for p in (1, 2, 0):
        third_finish(p)

    for copy in sent:
        copy.wait_send()

    @pl.loop(0, 8)
    def _(u):
        half_copy(u).wait_send()

    assert count[0] <= MESSAGES


def project(dense, base_mass, iface_modes):
    hbm = pl.BlockSpec(memory_space=pl.ANY)
    return pl.pallas_call(
        project_kernel,
        out_shape=jax.ShapeDtypeStruct((256, 128), F32),
        in_specs=[hbm, hbm, hbm],
        out_specs=pl.BlockSpec(memory_space=pltpu.VMEM),
        scratch_shapes=list(SCRATCH.values()),
        compiler_params=pltpu.CompilerParams(
            collective_id=0, has_side_effects=True, vmem_limit_bytes=67043328
        ),
    )(dense, base_mass, iface_modes)


def on_device(modes, coupling, inv_eig, sub_rows, adjacency, base_mass, iface_modes):
    dense = contributions(modes, coupling, inv_eig, sub_rows, adjacency)
    return project(dense, base_mass, iface_modes)


def solution(mesh):
    placed = (
        P(("sub", "tile"), None, None),
        P(("sub", "tile"), None, None, None),
        P(("sub", "tile"), None),
        P(("sub", "tile")),
        P(("sub", "tile"), None),
        P(("sub", "tile"), None, None),
        P(("sub", "tile"), None),
    )
    return jax.shard_map(
        on_device, mesh=mesh, in_specs=placed, out_specs=P("sub", "tile"), check_vma=False
    )
```
